256 devices in a mesh: dp: 64 (over x_lo, y, z), ep: 4 (over x_hi, core).
Axes of the slice: x: 4 (x_hi: 2, x_lo: 2; x = x_hi * 2 + x_lo), y: 4, z: 8, core: 2. Of those that a mesh axis runs over, the one named last changes fastest.
Arguments:
- tokens: bfloat16 [1024, 4096], P(('dp', 'ep')), may hold values from -6 to 6
- router: float32 [4096, 8], replicated, may hold values from -0.1875 to 0.1875
- expert_ids: int32 [1024, 2], P(('dp', 'ep')), may hold values from 0 to 7, all different within a row; in each aligned block of 4 rows (0 to 3, 4 to 7, ...) at most 2 rows name the same one
- w_gate: bfloat16 [64, 4096, 1536], P('dp', None, 'ep'), may hold values from -0.09375 to 0.09375
- w_up: bfloat16 [64, 4096, 1536], P('dp', None, 'ep'), may hold values from -0.09375 to 0.09375
- w_down: bfloat16 [64, 1536, 4096], P('dp', 'ep'), may hold values from -0.0546875 to 0.0546875
- states: bfloat16 [1024, 16, 8192], P('dp', None, 'ep'), may hold values from -6 to 6
- kv_blocks: bfloat16 [2048, 2, 16, 1024], P('dp', None, None, 'ep'), may hold values from -6 to 6
- plan_slots: int32 [64, 2, 3], replicated, may hold values from -1 to 63, as said below
- plan_len: int32 [64, 2], replicated, may hold values from 0 to 32, as said below
- plan_blocks: int32 [64, 2, 2, 2], replicated, may hold values from -1 to 31, as said below
Outputs:
- mixed: bfloat16 [1024, 4096], P(('dp', 'ep'))
- new_states: bfloat16 [1024, 16, 8192], P('dp', None, 'ep')
- new_cache: bfloat16 [2048, 2, 16, 1024], P('dp', None, None, 'ep')
The draws below stay inside these ranges and needn't reach their ends.
Inputs may be any that keep to these rules, and one draw needn't show every extreme that they name: `expert_ids`: in the rows of one device no expert is named more than 2 times. `plan_slots`: A move is live exactly where its first entry is not -1, and then all three entries are set; otherwise all are -1. For each m there is one distance d_m from 1 to 63, distinct for distinct m, such that every live move (r, m) goes to rank (r + d_m) mod 64. The leaving slots of a rank are distinct, the slots taken at a rank are distinct and differ from its leaving slots. Some rank has all 2 moves live. `plan_len`: zero exactly where the move is not live; some move holds 32 tokens. `plan_blocks`: entry j of both tables is -1 exactly where j * 16 >= plan_len. The blocks leaving a rank are distinct, the blocks taken at a rank are distinct and differ from the ones leaving it.
All inputs are finite; a program needn't handle non-finite values.
Results may differ from the reference program's by a relative error of at most 0.005.
Values may be sent and summed in bfloat16 or wider, within the bound.
No kernel may reach another device: no remote copies, remote signals or barrier semaphores. Data moves between devices by JAX's collectives and lax.ppermute only.
A program may use at most 128 MiB of HBM per device.

```python
import math
import jax
import jax.numpy as jnp
import numpy as np
from jax import lax

D = 4096
FF = 12288
EXPERTS = 8
CHANNELS = 8192
NST = 16
KVH = 8
HEAD = 128
BLK = 16
TOK_DEV = 4
SLOTS = 16
BLOCKS = 32
MOVE = 2
BPR = 2
CAP = 2
GROUP = 8
TOKENS = 1024
N_DP = 64
N_EP = 4


def plan_core(key):
    base = jax.random.fold_in(key, 4242)
    keys = jax.random.split(base, 7)
    offsets = 1 + jax.random.permutation(keys[1], N_DP - 1)[:MOVE]
    rank_line = jnp.arange(N_DP, dtype=jnp.int32)
    target_rank = ((rank_line[:, None] + offsets[None, :]) % N_DP).astype(jnp.int32)
    move_line = jnp.arange(MOVE, dtype=jnp.int32)
    live = jax.random.randint(keys[2], (N_DP, MOVE), 0, 5) < 3
    busiest = jax.random.randint(keys[3], (), 0, N_DP)
    live = live | (rank_line[:, None] == busiest)
    slot_perm = jax.vmap(lambda inner: jax.random.permutation(inner, SLOTS))(jax.random.split(keys[4], N_DP))
    block_perm = jax.vmap(lambda inner: jax.random.permutation(inner, BLOCKS))(jax.random.split(keys[5], N_DP))
    length = jax.random.randint(keys[6], (N_DP, MOVE), 1, BPR * BLK + 1)
    longest = (rank_line[:, None] == busiest) & (move_line[None, :] == 0)
    length = jnp.where(longest, BPR * BLK, length)
    length = jnp.where(live, length, 0).astype(jnp.int32)
    leaving_slot = jnp.where(live, slot_perm[:, :MOVE], -1)
    taken_slot = jnp.where(live, slot_perm[target_rank, MOVE + move_line[None, :]], -1)
    drawn_rank = jnp.where(live, target_rank, -1)
    plan_slots = jnp.stack([leaving_slot, drawn_rank, taken_slot], axis=-1).astype(jnp.int32)
    block_count = (length + BLK - 1) // BLK
    block_line = jnp.arange(BPR, dtype=jnp.int32)
    used = block_line[None, None, :] < block_count[:, :, None]
    leaving_block = block_perm[:, :MOVE * BPR].reshape(N_DP, MOVE, BPR)
    taken_block = block_perm[target_rank[:, :, None], MOVE * BPR + move_line[None, :, None] * BPR + block_line[None, None, :]]
    leaving_block = jnp.where(used, leaving_block, -1)
    taken_block = jnp.where(used, taken_block, -1)
    plan_blocks = jnp.stack([leaving_block, taken_block], axis=2).astype(jnp.int32)
    return (plan_slots, length, plan_blocks)


def draw_plan_slots(key, part):
    return plan_core(key)[0]


def draw_plan_len(key, part):
    return plan_core(key)[1]


def draw_plan_blocks(key, part):
    return plan_core(key)[2]


def levels(own_key, dims, shards, smallest, high):
    factor_of = 1.0
    for axis_at, shards_of in shards:
        draws = jax.random.uniform(jax.random.fold_in(jax.random.fold_in(own_key, 6), axis_at), (shards_of,), jnp.float32, smallest / len(shards), high / len(shards))
        factor_of = factor_of * jnp.repeat(jnp.exp(draws), dims[axis_at] // shards_of).reshape((-1,) + (1,) * (len(dims) - 1 - axis_at))
    return factor_of


def shared_out(key, own, number, rows, count, top, reach, skew):
    order = jax.random.permutation(key, count)
    heavy_load, usual = shares(count, rows * top, reach, skew, True), shares(count, rows * top, reach, skew, False)
    places = jnp.arange(count)

    def named(sizes, rotation):
        used = int((sizes > 0).sum())
        fixed = max(1, used // 4)
        passed = fixed + (places - fixed + rotation * (used - fixed)) % max(1, count - fixed)
        return jnp.zeros((count,), jnp.int32).at[order[jnp.where(places < fixed, places, passed)]].set(jnp.asarray(sizes, jnp.int32))

    sizes = jnp.where(number % 4 == 0, named(heavy_load, number // 4), named(usual, number - number // 4 - 1))
    mixed = jax.random.permutation(jax.random.fold_in(own, 3), count)
    giver, taker = mixed[0:count // 2 * 2:2], mixed[1:count // 2 * 2:2]
    margin = jnp.minimum(sizes[giver] - 1, reach - sizes[taker]) // 2
    margin = jnp.where((giver == order[0]) | (taker == order[0]) | (sizes[taker] == 0), 0, jnp.maximum(margin, 0))
    passed = jax.random.randint(jax.random.fold_in(own, 4), (count // 2,), 0, 1 << 20) % (margin + 1)
    sizes = sizes.at[giver].add(-passed).at[taker].add(passed)
    labels = jnp.searchsorted(jnp.cumsum(sizes), jnp.arange(rows * top), side="right").astype(jnp.int32)
    listing = labels.reshape(top, rows).T
    listing = listing[jax.random.permutation(jax.random.fold_in(own, 1), rows)]
    rotation = jax.random.randint(jax.random.fold_in(own, 2), (rows, 1), 0, top)
    return jnp.take_along_axis(listing, (jnp.arange(top)[None, :] + rotation) % top, axis=1)


def shares(number_of, total, reach, skew, full):
    weights = [(1 << 20) // math.isqrt(rank ** skew) + 1 for rank in range(1, number_of + 1)]
    largest = reach if full else min(reach, max(-(-total // number_of), total * weights[0] // sum(weights)))
    least = 1 if total - largest >= number_of - 1 else 0
    holding, rest = [largest] + [least] * (number_of - 1), total - largest - least * (number_of - 1)
    while rest > 0:
        movable = [i for i in range(1, number_of) if holding[i] < largest] or [i for i in range(1, number_of) if holding[i] < reach]
        whole, left = sum([weights[i] for i in movable]), rest
        for i in movable:
            addition = min(reach - holding[i], max(1, left * weights[i] // whole), rest)
            holding[i] = holding[i] + addition
            rest = rest - addition
    return np.array(holding)


def bell_draw(rng, shape, scale, limit, pieces=(), held_as=jnp.bfloat16):
    values = scale * jax.random.normal(rng, shape, jnp.float32)
    if pieces:
        values = values * levels(rng, shape, pieces, -0.22, 0.18)
    return jnp.clip(values, -limit, limit).astype(held_as)


def setup_inputs(seed: int = 0) -> dict:
    streams_of = jax.random.split(jax.random.key(seed), 12)
    tokens = bell_draw(streams_of[0], (TOKENS, D), 1.0, 6.0, ((0, 256),))
    router = bell_draw(streams_of[1], (D, EXPERTS), (D // 4) ** -0.5, 0.1875, (), jnp.float32)
    expert_ids_keys = jax.random.split(jax.random.fold_in(streams_of[2], 1), TOKENS // TOK_DEV)
    expert_ids_turns = jax.random.permutation(jax.random.fold_in(streams_of[2], 3), TOKENS // TOK_DEV)
    expert_ids = jax.vmap(lambda own, number: shared_out(jax.random.fold_in(streams_of[2], 2), own, number, TOK_DEV, EXPERTS, 2, CAP, 2))(expert_ids_keys, expert_ids_turns).reshape((TOKENS, 2))
    w_gate = bell_draw(streams_of[3], (EXPERTS * GROUP, D, FF // GROUP), D ** -0.5, 0.09375, ((0, 64), (2, 4)))
    w_up = bell_draw(streams_of[4], (EXPERTS * GROUP, D, FF // GROUP), D ** -0.5, 0.09375, ((0, 64), (2, 4)))
    w_down = bell_draw(streams_of[5], (EXPERTS * GROUP, FF // GROUP, D), FF ** -0.5, 0.0546875, ((0, 64), (1, 4)))
    states = bell_draw(streams_of[6], (N_DP * SLOTS, NST, CHANNELS), 1.0, 6.0, ((0, 64), (2, 4)))
    kv_blocks = bell_draw(streams_of[7], (N_DP * BLOCKS, 2, BLK, KVH * HEAD), 1.0, 6.0, ((0, 64), (3, 4)))
    plan_slots = draw_plan_slots(jax.random.fold_in(streams_of[11], 71), 0)
    plan_len = draw_plan_len(jax.random.fold_in(streams_of[11], 71), 0)
    plan_blocks = draw_plan_blocks(jax.random.fold_in(streams_of[11], 71), 0)
    return dict(tokens=tokens, router=router, expert_ids=expert_ids, w_gate=w_gate, w_up=w_up, w_down=w_down, states=states, kv_blocks=kv_blocks, plan_slots=plan_slots, plan_len=plan_len, plan_blocks=plan_blocks)


def reference(tokens, router, expert_ids, w_gate, w_up, w_down, states, kv_blocks, plan_slots, plan_len, plan_blocks):
    devices_all = N_DP * N_EP
    block_tokens = tokens.reshape(devices_all, TOK_DEV, D)
    pick_ids = expert_ids.reshape(devices_all, TOK_DEV * 2).astype(jnp.int32)
    onehot = (pick_ids[:, :, None] == jnp.arange(EXPERTS, dtype=jnp.int32)[None, None, :]).astype(jnp.int32)
    earlier = jnp.cumsum(onehot, axis=1) - onehot
    slot_of = jnp.sum(earlier * onehot, axis=2).astype(jnp.int32)
    target_row = (pick_ids * CAP + slot_of).astype(jnp.int32)
    doubled = jnp.repeat(block_tokens, 2, axis=1)
    device_line = jnp.broadcast_to(jnp.arange(devices_all, dtype=jnp.int32)[:, None], target_row.shape)
    packed = jnp.zeros((devices_all, EXPERTS * CAP, D), tokens.dtype)
    packed = packed.at[device_line.reshape(-1), target_row.reshape(-1)].set(doubled.reshape(-1, D))
    expert_rows = packed.reshape(devices_all, EXPERTS, CAP, D).transpose(1, 0, 2, 3).reshape(EXPERTS, devices_all * CAP, D)
    slab_width = FF // GROUP
    gate_all = w_gate.reshape(EXPERTS, GROUP, D, slab_width)
    up_all = w_up.reshape(EXPERTS, GROUP, D, slab_width)
    down_all = w_down.reshape(EXPERTS, GROUP * slab_width, D)

    def run_expert(operands):
        rows, gate_slabs, up_slabs, down_matrix = operands
        gate_matrix = gate_slabs.transpose(1, 0, 2).reshape(D, FF)
        up_matrix = up_slabs.transpose(1, 0, 2).reshape(D, FF)
        gate = jnp.dot(rows, gate_matrix, preferred_element_type=jnp.float32)
        upper = jnp.dot(rows, up_matrix, preferred_element_type=jnp.float32)
        hidden = (jax.nn.silu(gate) * upper).astype(jnp.bfloat16)
        return jnp.dot(hidden, down_matrix, preferred_element_type=jnp.float32)

    expert_out = lax.map(run_expert, (expert_rows, gate_all, up_all, down_all))
    expert_out = expert_out.reshape(EXPERTS, devices_all, CAP, D)
    chosen = expert_out[pick_ids, device_line, slot_of]
    chosen = chosen.reshape(TOKENS, 2, D)
    logits = jnp.dot(tokens.astype(jnp.float32), router, precision=lax.Precision.HIGHEST)
    scores = jax.nn.sigmoid(jnp.take_along_axis(logits, expert_ids.astype(jnp.int32), axis=1))
    weights = scores / jnp.sum(scores, axis=1, keepdims=True)
    mixed = jnp.sum(weights[:, :, None] * chosen, axis=1).astype(jnp.bfloat16)

    rank_line = jnp.arange(N_DP, dtype=jnp.int32)
    slot_states = states.reshape(N_DP, SLOTS, NST, CHANNELS)
    leaving_slot = plan_slots[:, :, 0].astype(jnp.int32)
    target_rank = plan_slots[:, :, 1].astype(jnp.int32)
    target_slot = plan_slots[:, :, 2].astype(jnp.int32)
    gone = jnp.any(leaving_slot[:, :, None] == jnp.arange(SLOTS, dtype=jnp.int32)[None, None, :], axis=1)
    payload = slot_states[rank_line[:, None], jnp.maximum(leaving_slot, 0)]
    payload = jnp.where((leaving_slot >= 0)[:, :, None, None], payload, jnp.zeros_like(payload))
    new_states = jnp.where(gone[:, :, None, None], jnp.zeros_like(slot_states), slot_states)
    rank_index = jnp.where(target_rank >= 0, target_rank, N_DP).astype(jnp.int32)
    slot_index = jnp.maximum(target_slot, 0).astype(jnp.int32)
    new_states = new_states.at[rank_index.reshape(-1), slot_index.reshape(-1)].set(payload.reshape(-1, NST, CHANNELS), mode="drop")
    new_states = new_states.reshape(N_DP * SLOTS, NST, CHANNELS)

    cache = kv_blocks.reshape(N_DP, BLOCKS, 2, BLK, KVH * HEAD)
    leaving_block = plan_blocks[:, :, 0, :].astype(jnp.int32)
    taken_block = plan_blocks[:, :, 1, :].astype(jnp.int32)
    gone_blocks = jnp.any(leaving_block.reshape(N_DP, -1)[:, :, None] == jnp.arange(BLOCKS, dtype=jnp.int32)[None, None, :], axis=1)
    cache_payload = cache[rank_line[:, None, None], jnp.maximum(leaving_block, 0)]
    position = jnp.arange(BPR, dtype=jnp.int32)[:, None] * BLK + jnp.arange(BLK, dtype=jnp.int32)[None, :]
    written = (leaving_block >= 0)[:, :, :, None] & (position[None, None] < plan_len.astype(jnp.int32)[:, :, None, None])
    cache_payload = jnp.where(written[:, :, :, None, :, None], cache_payload, jnp.zeros_like(cache_payload))
    new_cache = jnp.where(gone_blocks[:, :, None, None, None], jnp.zeros_like(cache), cache)
    block_rank = jnp.where(taken_block >= 0, jnp.broadcast_to(target_rank[:, :, None], taken_block.shape), N_DP).astype(jnp.int32)
    block_index = jnp.maximum(taken_block, 0).astype(jnp.int32)
    new_cache = new_cache.at[block_rank.reshape(-1), block_index.reshape(-1)].set(cache_payload.reshape(-1, 2, BLK, KVH * HEAD), mode="drop")
    new_cache = new_cache.reshape(N_DP * BLOCKS, 2, BLK, KVH * HEAD)
    return mixed, new_states, new_cache
```

```python
import functools

import jax
import jax.numpy as jnp
from jax import lax
from jax.experimental import pallas as pl
from jax.experimental.pallas import tpu as pltpu
from jax.sharding import Mesh, PartitionSpec as P

CAP = 2
XL, Y, Z, XH, C = 2, 4, 8, 2, 2
RANK = ("xl", "y", "z")
COLUMN = ("xl", "y", "xh")


def passed(value, axis, steps):
    count = lax.axis_size(axis)
    pairs = [(source, (source + steps) % count) for source in range(count)]
    return lax.ppermute(value, axis, pairs)


def shifted(value, digit, unit, ranks):
    def branch(steps):
        pairs = [(source, (source + steps * unit) % ranks) for source in range(ranks)]
        return lambda item: lax.ppermute(item, RANK, pairs)

    return lax.switch(digit, [lambda item: item] + [branch(steps) for steps in range(1, 8)], value)


def leave_kernel(here, slots, blocks, s0, s1, k00, k01, k10, k11, out0, out1):
    for state, cache, out in ((s0, (k00, k01), out0), (s1, (k10, k11), out1)):
        channels = state.shape[2]
        out[:, :channels] = state[0]
        at = channels
        for block in cache:
            for k in range(block.shape[1]):
                wide = block.shape[3]
                out[:, at : at + wide] = block[0, k]
                at += wide


def leaving(here, slots, blocks, states, kv_blocks):
    rows, channels = states.shape[1:]
    halves, block_len, wide = kv_blocks.shape[1:]

    def state_at(m):
        return pl.BlockSpec((1, rows, channels), lambda i, h, s, b: (jnp.maximum(s[h[0] * 6 + m * 3], 0), 0, 0))

    def block_at(m, j):
        return pl.BlockSpec(
            (1, halves, block_len, wide),
            lambda i, h, s, b: (jnp.maximum(b[h[0] * 8 + m * 4 + j], 0), 0, 0, 0),
        )

    packed = (rows, channels + 2 * halves * wide)
    return pl.pallas_call(
        leave_kernel,
        out_shape=[jax.ShapeDtypeStruct(packed, states.dtype)] * 2,
        grid_spec=pltpu.PrefetchScalarGridSpec(
            num_scalar_prefetch=3,
            grid=(1,),
            in_specs=[state_at(0), state_at(1), block_at(0, 0), block_at(0, 1), block_at(1, 0), block_at(1, 1)],
            out_specs=[pl.BlockSpec(packed, lambda i, h, s, b: (0, 0))] * 2,
        ),
        name="leave",
    )(here, slots, blocks, states, states, kv_blocks, kv_blocks, kv_blocks, kv_blocks)


def land_kernel(ranks, here, far, slots, blocks, lens, states, cache, pay0, pay1, new_states, new_cache):
    me = here[0]
    channels = states.shape[2]
    halves, block_len, wide = cache.shape[1:]
    new_states[...] = states[...]
    new_cache[...] = cache[...]
    for m in range(2):
        slot = slots[me * 6 + m * 3]

        @pl.when(slot >= 0)
        def _(slot=slot):
            new_states[slot] = jnp.zeros(states.shape[1:], states.dtype)

        for j in range(2):
            block = blocks[me * 8 + m * 4 + j]

            @pl.when(block >= 0)
            def _(block=block):
                new_cache[block] = jnp.zeros(cache.shape[1:], cache.dtype)

    for m, pay in enumerate((pay0, pay1)):
        sender = lax.rem(me - far[m] + ranks, ranks)
        live = slots[sender * 6 + m * 3] >= 0
        place = slots[sender * 6 + m * 3 + 2]
        length = lens[sender * 2 + m]

        @pl.when(live)
        def _(pay=pay, place=place):
            new_states[place] = pay[:, :channels]

        for j in range(2):
            spot = blocks[sender * 8 + m * 4 + 2 + j]

            @pl.when(live & (spot >= 0))
            def _(pay=pay, spot=spot, j=j, length=length):
                row = lax.broadcasted_iota(jnp.int32, (block_len, wide), 0) + j * block_len
                for k in range(halves):
                    at = channels + (j * halves + k) * wide
                    block = pay[:, at : at + wide]
                    new_cache[spot, k] = jnp.where(row < length, block, jnp.zeros_like(block))


def landing(here, far, slots, blocks, lens, states, kv_blocks, pay0, pay1, ranks):
    whole = [states, kv_blocks, pay0, pay1]

    def all_of(item):
        return pl.BlockSpec(item.shape, lambda i, *_: (0,) * item.ndim)

    return pl.pallas_call(
        functools.partial(land_kernel, ranks),
        out_shape=[jax.ShapeDtypeStruct(v.shape, v.dtype) for v in (states, kv_blocks)],
        grid_spec=pltpu.PrefetchScalarGridSpec(
            num_scalar_prefetch=5,
            grid=(1,),
            in_specs=[all_of(v) for v in whole],
            out_specs=[all_of(states), all_of(kv_blocks)],
        ),
        name="land",
    )(here, far, slots, blocks, lens, *whole)


def plan_of(plan_slots, plan_len, plan_blocks):
    ranks = plan_slots.shape[0]
    here = lax.axis_index(RANK).astype(jnp.int32)
    rank_line = jnp.arange(ranks, dtype=jnp.int32)
    live = plan_slots[:, :, 0] >= 0
    span = jnp.where(live, (plan_slots[:, :, 1] - rank_line[:, None]) % ranks, 0)
    far = jnp.max(span, axis=0)
    return here.reshape(1), far, plan_slots.reshape(-1), plan_blocks.reshape(-1), plan_len.reshape(-1)


def expert_kernel(count, *refs):
    chunks, (gate_w, up_w, down_w, own, other) = refs[:count], refs[count:]
    rows = jnp.concatenate([chunk[...] for chunk in chunks], axis=0)
    gate = jnp.dot(rows, gate_w[0], preferred_element_type=jnp.float32)
    up = jnp.dot(rows, up_w[0], preferred_element_type=jnp.float32)
    hidden = (gate / (1 + jnp.exp(-gate)) * up).astype(jnp.bfloat16)
    half = own.shape[0]
    tile = 512
    for at in range(0, own.shape[1], tile):
        out = jnp.dot(hidden, down_w[0, :, at : at + tile], preferred_element_type=jnp.float32)
        own[:, at : at + tile] = out[:half]
        other[:, at : at + tile] = out[half:].astype(jnp.bfloat16)


def experts_of(mine, theirs, w_gate, w_up, w_down):
    chunks = list(mine) + list(theirs)
    part, width = chunks[0].shape
    units = w_gate.shape[2]
    half = part * len(mine)
    return pl.pallas_call(
        functools.partial(expert_kernel, len(chunks)),
        out_shape=[
            jax.ShapeDtypeStruct((half, width), jnp.float32),
            jax.ShapeDtypeStruct((half, width), jnp.bfloat16),
        ],
        in_specs=[pl.BlockSpec(memory_space=pltpu.VMEM)] * (len(chunks) + 3),
        out_specs=[pl.BlockSpec(memory_space=pltpu.VMEM)] * 2,
        compiler_params=pltpu.CompilerParams(vmem_limit_bytes=12 << 20),
        cost_estimate=pl.CostEstimate(
            flops=12 * half * width * units,
            transcendentals=2 * half * units,
            bytes_accessed=10 * half * width,
        ),
        name="experts",
    )(*chunks, w_gate, w_up, w_down)


def fetch_kernel(*refs):
    count = len(refs) // 2
    sems = refs[-1]
    copies = [pltpu.make_async_copy(refs[i], refs[count + i], sems.at[i]) for i in range(count)]
    for copy in copies:
        copy.start()
    for copy in copies:
        copy.wait()


def fetched(*weights):
    return pl.pallas_call(
        fetch_kernel,
        out_shape=[pltpu.VMEM(w.shape, w.dtype) for w in weights],
        in_specs=[pl.BlockSpec(memory_space=pltpu.HBM)] * len(weights),
        out_specs=[pl.BlockSpec(memory_space=pltpu.VMEM)] * len(weights),
        scratch_shapes=[pltpu.SemaphoreType.DMA((len(weights),))],
        compiler_params=pltpu.CompilerParams(vmem_limit_bytes=12 << 20),
        name="fetch",
    )(*weights)


def local(
    tokens, router, expert_ids, w_gate, w_up, w_down, states, kv_blocks, plan_slots, plan_len, plan_blocks
):
    experts = router.shape[1]
    tok_count, width = tokens.shape
    f32, bf16 = jnp.float32, jnp.bfloat16
    here, far, slots, blocks, lens = plan_of(plan_slots, plan_len, plan_blocks)
    ranks = plan_slots.shape[0]
    pay0, pay1 = leaving(here, slots, blocks, states, kv_blocks)

    flat_ids = expert_ids.reshape(-1)
    onehot = (flat_ids[:, None] == jnp.arange(experts)[None, :]).astype(jnp.int32)
    earlier = jnp.cumsum(onehot, axis=0) - onehot
    slot_of = jnp.sum(earlier * onehot, axis=1)
    target_row = flat_ids * CAP + slot_of
    placer = (jnp.arange(experts * CAP)[:, None] == target_row[None, :]).astype(bf16)
    doubled = jnp.repeat(tokens, 2, axis=0)
    packed = jnp.dot(placer, doubled, preferred_element_type=f32).astype(bf16)
    outgoing = jnp.repeat(packed.reshape(experts, CAP, width), XH, axis=0)
    outgoing, pay0, pay1, w_gate, w_up, w_down = lax.optimization_barrier(
        (outgoing, pay0, pay1, w_gate, w_up, w_down)
    )
    own = lax.all_to_all(outgoing, COLUMN, split_axis=0, concat_axis=0, tiled=True)
    w_gate, w_up, w_down = fetched(w_gate, w_up, w_down)
    own, w_gate, w_up, w_down = lax.optimization_barrier((own, w_gate, w_up, w_down))
    own = own.reshape(-1, width)
    part = own.shape[0]
    kept, back = {}, {}

    def run_experts(names, mine):
        theirs = [passed(chunk, "c", 1) for chunk in mine]
        ours, sent = experts_of(mine, theirs, w_gate, w_up, w_down)
        sent = passed(sent, "c", 1)
        for i, name in enumerate(names):
            kept[name] = ours[i * part : (i + 1) * part]
            back[name] = sent[i * part : (i + 1) * part]
        return ours

    down, up = passed(own, "z", 1), passed(own, "z", -1)
    done = run_experts([0], [own])
    for step in range(1, Z // 2):
        down, up, done = lax.optimization_barrier((down, up, done))
        below, above = down, up
        down = passed(down, "z", 1)
        if step < Z // 2 - 1:
            up = passed(up, "z", -1)
        done = run_experts([-step, step], [below, above])
    down, done = lax.optimization_barrier((down, done))
    run_experts([-Z // 2], [down])

    def with_sum(value, name):
        return (value + kept[name] + back[name].astype(f32)).astype(bf16)

    left, right = with_sum(0, -Z // 2), with_sum(0, Z // 2 - 1)
    pays = [pay0, pay1]
    hops = [(0, 8), (1, 8), (0, 1), (1, 1)]
    for d, (m, unit) in zip(range(Z // 2 - 1, -1, -1), hops):
        left, right, pay = lax.optimization_barrier((left, right, pays[m]))
        left = passed(left, "z", -1)
        if d:
            right = passed(right, "z", 1)
        pays[m] = shifted(pay, far[m] // 8 if unit == 8 else far[m] % 8, unit, ranks)
        left, pays[m] = lax.optimization_barrier((left, pays[m]))
        if d:
            left = with_sum(left.astype(f32), -d)
            if d > 1:
                right = with_sum(right.astype(f32), d - 1)
    total = with_sum(left.astype(f32) + right.astype(f32), 0)
    pay0, pay1 = pays
    new_states, new_cache = landing(here, far, slots, blocks, lens, states, kv_blocks, pay0, pay1, ranks)
    returned = lax.all_to_all(
        total.reshape(experts * XH, CAP, width), COLUMN, split_axis=0, concat_axis=0, tiled=True
    )
    expert_out = jnp.sum(returned.reshape(experts, XH, CAP, width).astype(f32), axis=1).reshape(experts * CAP, width)
    chosen = expert_out[target_row].reshape(tok_count, 2, width)
    logits = jnp.dot(tokens.astype(f32), router, precision=lax.Precision.HIGHEST)
    scores = jax.nn.sigmoid(jnp.take_along_axis(logits, expert_ids, axis=1))
    weights = scores / jnp.sum(scores, axis=1, keepdims=True)
    mixed = jnp.sum(weights[:, :, None] * chosen, axis=1).astype(bf16)
    return mixed, new_states, new_cache


def solution(mesh):
    fine = Mesh(mesh.devices.reshape(XL, Y, Z, XH, C), ("xl", "y", "z", "xh", "c"))
    inner = ("xh", "c")
    everyone = RANK + inner
    placed = (
        P(everyone, None),
        P(),
        P(everyone, None),
        P(RANK, None, inner),
        P(RANK, None, inner),
        P(RANK, inner, None),
        P(RANK, None, inner),
        P(RANK, None, None, inner),
        P(),
        P(),
        P(),
    )
    return jax.shard_map(
        local,
        mesh=fine,
        in_specs=placed,
        out_specs=(P(everyone, None), P(RANK, None, inner), P(RANK, None, None, inner)),
        check_vma=False,
    )
```

```python
import functools
import math

import jax
import jax.numpy as jnp
from jax import lax
from jax.experimental import pallas as pl
from jax.experimental.pallas import tpu as pltpu
from jax.sharding import Mesh, PartitionSpec as P

CAP = 2
XL, Y, Z, XH, C = 2, 4, 8, 2, 2
RANK = ("xl", "y", "z")
COLUMN = ("xl", "y", "xh")


def passed(value, axis, steps):
    count = math.prod(lax.axis_size(name) for name in axis) if isinstance(axis, tuple) else lax.axis_size(axis)
    pairs = [(source, (source + steps) % count) for source in range(count)]
    return lax.ppermute(value, axis, pairs)


def leave_kernel(here, slots, blocks, s0, s1, k00, k01, k10, k11, out0, out1):
    for state, cache, out in ((s0, (k00, k01), out0), (s1, (k10, k11), out1)):
        channels = state.shape[2]
        out[:, :channels] = state[0]
        at = channels
        for block in cache:
            for k in range(block.shape[1]):
                wide = block.shape[3]
                out[:, at : at + wide] = block[0, k]
                at += wide


def leaving(here, slots, blocks, states, kv_blocks):
    rows, channels = states.shape[1:]
    halves, block_len, wide = kv_blocks.shape[1:]

    def state_at(m):
        return pl.BlockSpec((1, rows, channels), lambda i, h, s, b: (jnp.maximum(s[h[0] * 6 + m * 3], 0), 0, 0))

    def block_at(m, j):
        return pl.BlockSpec(
            (1, halves, block_len, wide),
            lambda i, h, s, b: (jnp.maximum(b[h[0] * 8 + m * 4 + j], 0), 0, 0, 0),
        )

    packed = (rows, channels + 2 * halves * wide)
    return pl.pallas_call(
        leave_kernel,
        out_shape=[jax.ShapeDtypeStruct(packed, states.dtype)] * 2,
        grid_spec=pltpu.PrefetchScalarGridSpec(
            num_scalar_prefetch=3,
            grid=(1,),
            in_specs=[state_at(0), state_at(1), block_at(0, 0), block_at(0, 1), block_at(1, 0), block_at(1, 1)],
            out_specs=[pl.BlockSpec(packed, lambda i, h, s, b: (0, 0))] * 2,
        ),
        name="leave",
    )(here, slots, blocks, states, states, kv_blocks, kv_blocks, kv_blocks, kv_blocks)


def clear_kernel(here, slots, blocks, states, cache, new_states, new_cache):
    me = here[0]
    new_states[...] = states[...]
    new_cache[...] = cache[...]
    for m in range(2):
        slot = slots[me * 6 + m * 3]

        @pl.when(slot >= 0)
        def _(slot=slot):
            new_states[slot] = jnp.zeros(states.shape[1:], states.dtype)

        for j in range(2):
            block = blocks[me * 8 + m * 4 + j]

            @pl.when(block >= 0)
            def _(block=block):
                new_cache[block] = jnp.zeros(cache.shape[1:], cache.dtype)


def cleared(here, slots, blocks, states, kv_blocks):
    def all_of(item):
        return pl.BlockSpec(item.shape, lambda i, *_: (0,) * item.ndim)

    return pl.pallas_call(
        clear_kernel,
        out_shape=[jax.ShapeDtypeStruct(v.shape, v.dtype) for v in (states, kv_blocks)],
        grid_spec=pltpu.PrefetchScalarGridSpec(
            num_scalar_prefetch=3,
            grid=(1,),
            in_specs=[all_of(states), all_of(kv_blocks)],
            out_specs=[all_of(states), all_of(kv_blocks)],
        ),
        compiler_params=pltpu.CompilerParams(vmem_limit_bytes=16 << 20),
        name="clear",
    )(here, slots, blocks, states, kv_blocks)


def plan_of(plan_slots, plan_len, plan_blocks):
    ranks = plan_slots.shape[0]
    here = lax.axis_index(RANK).astype(jnp.int32)
    rank_line = jnp.arange(ranks, dtype=jnp.int32)
    live = plan_slots[:, :, 0] >= 0
    span = jnp.where(live, (plan_slots[:, :, 1] - rank_line[:, None]) % ranks, 0)
    far = jnp.max(span, axis=0)
    return here.reshape(1), far, plan_slots.reshape(-1), plan_blocks.reshape(-1), plan_len.reshape(-1)


def patch_kernel(ranks, here, far, slots, blocks, lens, pay0, pay1, _, __, new_states, new_cache, kept, sems):
    channels = new_states.shape[2]
    halves, block_len, wide = new_cache.shape[1:]
    row = lax.broadcasted_iota(jnp.int32, (block_len, wide), 0)
    moves = []
    for m, pay in enumerate((pay0, pay1)):
        sender = lax.rem(here[0] - far[m] + ranks, ranks)
        live = slots[sender * 6 + m * 3] >= 0
        place = jnp.where(live, slots[sender * 6 + m * 3 + 2], 0)
        length = lens[sender * 2 + m]
        copy = pltpu.make_async_copy(pay.at[:, pl.ds(0, channels)], new_states.at[place], sems.at[m * 3])
        moves.append((live, copy))
        pl.when(live)(copy.start)
        for j in range(2):
            spot = blocks[sender * 8 + m * 4 + 2 + j]
            held = live & (spot >= 0)
            for k in range(halves):
                at = channels + (j * halves + k) * wide
                block = pay[:, at : at + wide]
                kept[m * 2 + j, k] = jnp.where(row + j * block_len < length, block, jnp.zeros_like(block))
            copy = pltpu.make_async_copy(
                kept.at[m * 2 + j], new_cache.at[jnp.where(held, spot, 0)], sems.at[m * 3 + 1 + j]
            )
            moves.append((held, copy))
            pl.when(held)(copy.start)
    for held, copy in moves:
        pl.when(held)(copy.wait)


def patched(here, far, slots, blocks, lens, pay0, pay1, new_states, new_cache, ranks):
    anywhere = pl.BlockSpec(memory_space=pltpu.HBM)
    payload = pl.BlockSpec(pay0.shape, lambda i, *_: (0, 0))
    return pl.pallas_call(
        functools.partial(patch_kernel, ranks),
        out_shape=[jax.ShapeDtypeStruct(v.shape, v.dtype) for v in (new_states, new_cache)],
        grid_spec=pltpu.PrefetchScalarGridSpec(
            num_scalar_prefetch=5,
            grid=(1,),
            in_specs=[payload, payload, anywhere, anywhere],
            out_specs=[anywhere, anywhere],
            scratch_shapes=[pltpu.VMEM((4,) + new_cache.shape[1:], new_cache.dtype), pltpu.SemaphoreType.DMA((6,))],
        ),
        input_output_aliases={7: 0, 8: 1},
        name="patch",
    )(here, far, slots, blocks, lens, pay0, pay1, new_states, new_cache)


def rows_kernel(blocks, rows):
    for i in range(blocks.shape[0]):
        rows[CAP * i : CAP * (i + 1)] = blocks[i]


def rows_from(blocks):
    count, cap, width = blocks.shape
    return pl.pallas_call(
        rows_kernel,
        out_shape=jax.ShapeDtypeStruct((count * cap, width), blocks.dtype),
        in_specs=[pl.BlockSpec(memory_space=pltpu.VMEM)],
        out_specs=pl.BlockSpec(memory_space=pltpu.VMEM),
        compiler_params=pltpu.CompilerParams(vmem_limit_bytes=12 << 20),
        name="rows",
    )(blocks)


def sum_kernel(count, kept, back, *refs):
    total = kept[...] + back[...].astype(jnp.float32)
    for i in range(count):
        total = total + refs[i][...].astype(jnp.float32)
    total = total.astype(jnp.bfloat16)
    out = refs[count]
    if len(out.shape) == 2:
        out[...] = total
    else:
        for i in range(out.shape[0]):
            out[i] = total[CAP * i : CAP * (i + 1)]


def summed(kept, back, at, rows, *arrived, blocks=False):
    width = kept.shape[1]
    piece = pl.BlockSpec((rows, width), lambda i: (at, 0))
    whole = pl.BlockSpec((rows, width), lambda i: (0, 0))
    shape = (rows // CAP, CAP, width) if blocks else (rows, width)
    return pl.pallas_call(
        functools.partial(sum_kernel, len(arrived)),
        out_shape=jax.ShapeDtypeStruct(shape, jnp.bfloat16),
        grid=(1,),
        in_specs=[piece, piece] + [whole] * len(arrived),
        out_specs=pl.BlockSpec(shape, lambda i: (0,) * len(shape)),
        compiler_params=pltpu.CompilerParams(vmem_limit_bytes=12 << 20),
        name="sums",
    )(kept, back, *arrived)


def mix_kernel(rows, weights, returned, out):
    mixed = []
    for t in range(out.shape[0]):
        total = 0
        for k in range(2):
            row = rows[2 * t + k]
            e, slot = row // CAP, row % CAP
            both = returned[XH * e].astype(jnp.float32)
            for x in range(1, XH):
                both = both + returned[XH * e + x].astype(jnp.float32)
            picked = jnp.where(slot == 0, both[0:1], both[1:2])
            total = total + weights[2 * t + k] * picked
        mixed.append(total)
    out[...] = jnp.concatenate(mixed, axis=0).astype(out.dtype)


def mixed_of(rows, weights, returned, count):
    width = returned.shape[2]
    return pl.pallas_call(
        mix_kernel,
        out_shape=jax.ShapeDtypeStruct((count, width), returned.dtype),
        in_specs=[pl.BlockSpec(memory_space=pltpu.SMEM)] * 2 + [pl.BlockSpec(memory_space=pltpu.VMEM)],
        out_specs=pl.BlockSpec(memory_space=pltpu.VMEM),
        compiler_params=pltpu.CompilerParams(vmem_limit_bytes=12 << 20),
        name="mix",
    )(rows, weights, returned)


def expert_kernel(count, *refs):
    chunks, (gate_w, up_w, down_w, own, other) = refs[:count], refs[count:]
    rows = jnp.concatenate([chunk[...] for chunk in chunks], axis=0)
    gate = jnp.dot(rows, gate_w[0], preferred_element_type=jnp.float32)
    up = jnp.dot(rows, up_w[0], preferred_element_type=jnp.float32)
    hidden = (gate / (1 + jnp.exp(-gate)) * up).astype(jnp.bfloat16)
    half = own.shape[0]
    tile = 512
    for at in range(0, own.shape[1], tile):
        out = jnp.dot(hidden, down_w[0, :, at : at + tile], preferred_element_type=jnp.float32)
        own[:, at : at + tile] = out[:half]
        other[:, at : at + tile] = out[half:].astype(jnp.bfloat16)


def experts_of(mine, theirs, w_gate, w_up, w_down):
    chunks = list(mine) + list(theirs)
    part, width = chunks[0].shape
    units = w_gate.shape[2]
    half = part * len(mine)
    return pl.pallas_call(
        functools.partial(expert_kernel, len(chunks)),
        out_shape=[
            jax.ShapeDtypeStruct((half, width), jnp.float32),
            jax.ShapeDtypeStruct((half, width), jnp.bfloat16),
        ],
        grid=(1,),
        in_specs=[pl.BlockSpec(memory_space=pltpu.VMEM)] * (len(chunks) + 3),
        out_specs=[pl.BlockSpec((half, width), lambda i: (0, 0))] * 2,
        compiler_params=pltpu.CompilerParams(vmem_limit_bytes=12 << 20),
        cost_estimate=pl.CostEstimate(
            flops=12 * half * width * units,
            transcendentals=2 * half * units,
            bytes_accessed=10 * half * width,
        ),
        name="experts",
    )(*chunks, w_gate, w_up, w_down)


def fetch_kernel(*refs):
    count = len(refs) // 2
    sems = refs[-1]
    copies = [pltpu.make_async_copy(refs[i], refs[count + i], sems.at[i]) for i in range(count)]
    for copy in copies:
        copy.start()
    for copy in copies:
        copy.wait()


def fetched(*weights):
    return pl.pallas_call(
        fetch_kernel,
        out_shape=[pltpu.VMEM(w.shape, w.dtype) for w in weights],
        in_specs=[pl.BlockSpec(memory_space=pltpu.HBM)] * len(weights),
        out_specs=[pl.BlockSpec(memory_space=pltpu.VMEM)] * len(weights),
        scratch_shapes=[pltpu.SemaphoreType.DMA((len(weights),))],
        compiler_params=pltpu.CompilerParams(vmem_limit_bytes=44 << 20),
        name="fetch",
    )(*weights)


def local(
    tokens, router, expert_ids, w_gate, w_up, w_down, states, kv_blocks, plan_slots, plan_len, plan_blocks
):
    experts = router.shape[1]
    tok_count, width = tokens.shape
    f32, bf16 = jnp.float32, jnp.bfloat16
    here, far, slots, blocks, lens = plan_of(plan_slots, plan_len, plan_blocks)
    ranks = plan_slots.shape[0]
    flat_ids = expert_ids.reshape(-1)
    onehot = (flat_ids[:, None] == jnp.arange(experts)[None, :]).astype(jnp.int32)
    earlier = jnp.cumsum(onehot, axis=0) - onehot
    slot_of = jnp.sum(earlier * onehot, axis=1)
    target_row = flat_ids * CAP + slot_of
    placer = (jnp.arange(experts * CAP)[:, None] == target_row[None, :]).astype(bf16)
    doubled = jnp.repeat(tokens, 2, axis=0)
    packed = jnp.dot(placer, doubled, preferred_element_type=f32).astype(bf16)
    outgoing = jnp.repeat(packed.reshape(experts, CAP, width), XH, axis=0)
    own = lax.all_to_all(outgoing, COLUMN, split_axis=0, concat_axis=0, tiled=True)
    moving = jnp.concatenate(leaving(here, slots, blocks, states, kv_blocks), axis=0)
    half = moving.shape[0] // 2
    steps_z, steps_xy = far % Z, far // Z

    def placed_at(value, places, count):
        line = jnp.arange(count)[:, None, None]
        rows = jnp.repeat(places, half)[None, :, None]
        return jnp.where(line == rows, value[None], jnp.zeros_like(value)[None]).reshape(-1, value.shape[1])

    at_z, at_xy = lax.axis_index("z"), lax.axis_index(("xl", "y"))
    moving = placed_at(moving, (at_z + steps_z) % Z, Z)
    own, moving = lax.optimization_barrier((own, moving))
    own = rows_from(own)
    part = own.shape[0]
    own, w_gate, w_up, w_down = lax.optimization_barrier((own, w_gate, w_up, w_down))
    moving = lax.psum_scatter(moving, "z", scatter_dimension=0, tiled=True)
    kept = {}

    def run_experts(names, mine):
        theirs = [passed(chunk, "c", 1) for chunk in mine]
        ours, sent = experts_of(mine, theirs, w_gate, w_up, w_down)
        sent = passed(sent, "c", 1)
        ours, sent = (pltpu.with_memory_space_constraint(v, pltpu.HBM) for v in (ours, sent))
        for i, name in enumerate(names):
            kept[name] = (ours, sent, i, part)
        return ours

    down, up = passed(own, "z", 1), passed(own, "z", -1)
    w_gate, w_up, w_down = fetched(w_gate, w_up, w_down)
    done = run_experts([0], [own])
    waiting = []
    for step in range(1, Z // 2 + 1):
        down, done = lax.optimization_barrier((down, done))
        names, chunks = [-step] + [name for name, _ in waiting], [down] + [chunk for _, chunk in waiting]
        if step < Z // 2:
            down = passed(down, "z", 1)
        done = run_experts(names, chunks)
        if step < Z // 2:
            up, done = lax.optimization_barrier((up, done))
            waiting = [(step, up)]
            if step < Z // 2 - 1:
                up = passed(up, "z", -1)

    left, right = summed(*kept[-Z // 2]), summed(*kept[Z // 2 - 1])
    left, moving = lax.optimization_barrier((left, moving))
    wrapped = (at_z < steps_z).astype(jnp.int32)
    moving = placed_at(moving, (at_xy + steps_xy + wrapped) % (XL * Y), XL * Y)
    moving = lax.psum_scatter(moving, ("xl", "y"), scatter_dimension=0, tiled=True)
    for d in range(Z // 2 - 1, -1, -1):
        left = passed(left, "z", -1)
        if d:
            left = summed(*kept[-d], left)
            right = passed(right, "z", 1)
            if d > 1:
                right = summed(*kept[d - 1], right)
    total = summed(*kept[0], left, right, blocks=True)
    new_states, new_cache = cleared(here, slots, blocks, states, kv_blocks)
    returned = lax.all_to_all(
        total, COLUMN, split_axis=0, concat_axis=0, tiled=True
    )
    pay0, pay1 = moving[:half], moving[half:]
    new_states, new_cache = patched(here, far, slots, blocks, lens, pay0, pay1, new_states, new_cache, ranks)
    logits = jnp.dot(tokens.astype(f32), router, precision=lax.Precision.HIGHEST)
    scores = jax.nn.sigmoid(jnp.take_along_axis(logits, expert_ids, axis=1))
    weights = scores / jnp.sum(scores, axis=1, keepdims=True)
    mixed = mixed_of(target_row, weights.reshape(-1), returned, tok_count)
    return mixed, new_states, new_cache


def solution(mesh):
    fine = Mesh(mesh.devices.reshape(XL, Y, Z, XH, C), ("xl", "y", "z", "xh", "c"))
    inner = ("xh", "c")
    everyone = RANK + inner
    placed = (
        P(everyone, None),
        P(),
        P(everyone, None),
        P(RANK, None, inner),
        P(RANK, None, inner),
        P(RANK, inner, None),
        P(RANK, None, inner),
        P(RANK, None, None, inner),
        P(),
        P(),
        P(),
    )
    return jax.shard_map(
        local,
        mesh=fine,
        in_specs=placed,
        out_specs=(P(everyone, None), P(RANK, None, inner), P(RANK, None, None, inner)),
        check_vma=False,
    )
```

```python
import functools
import math

import jax
import jax.numpy as jnp
from jax import lax
from jax.experimental import pallas as pl
from jax.experimental.pallas import tpu as pltpu
from jax.sharding import Mesh, PartitionSpec as P

CAP = 2
XL, Y, Z, XH, C = 2, 4, 8, 2, 2
RANK = ("xl", "y", "z")
COLUMN = ("xl", "y", "xh")


def passed(value, axis, steps):
    count = math.prod(lax.axis_size(name) for name in axis) if isinstance(axis, tuple) else lax.axis_size(axis)
    pairs = [(source, (source + steps) % count) for source in range(count)]
    return lax.ppermute(value, axis, pairs)


def sent_by(value, digit, ranks):
    def branch(steps):
        pairs = [(source, (source + steps) % ranks) for source in range(ranks)]
        return lambda item: lax.ppermute(item, RANK, pairs)

    return lax.switch(digit, [lambda item: item] + [branch(steps) for steps in range(1, Z)], value)


def leave_kernel(here, slots, blocks, s0, s1, k00, k01, k10, k11, out0, out1):
    channels = s0.shape[2]
    for state, cache, out in ((s0, (k00, k01), out0), (s1, (k10, k11), out1)):
        out[:, :channels] = state[0]
        at = channels
        for block in cache:
            for k in range(block.shape[1]):
                wide = block.shape[3]
                out[:, at : at + wide] = block[0, k]
                at += wide


def turn_kernel(bit, far, moved, moving, *outs):
    for m in range(2):
        taken = lax.rem(lax.div(far[m], bit), 2) == 1
        value = jnp.where(taken, moved[m], moving[m])
        if len(outs) == 2:
            outs[m][...] = value
        else:
            outs[0][m] = value


def turned_by(far, moved, moving, bit, apart):
    whole = jax.ShapeDtypeStruct(moving.shape, moving.dtype)
    single = jax.ShapeDtypeStruct(moving.shape[1:], moving.dtype)
    vmem = pl.BlockSpec(memory_space=pltpu.VMEM)
    return pl.pallas_call(
        functools.partial(turn_kernel, bit),
        out_shape=[single] * 2 if apart else whole,
        in_specs=[pl.BlockSpec(memory_space=pltpu.SMEM), vmem, vmem],
        out_specs=[vmem] * 2 if apart else vmem,
        compiler_params=pltpu.CompilerParams(vmem_limit_bytes=12 << 20),
        name="turn",
    )(far, moved, moving)


def leaving(here, slots, blocks, states, kv_blocks):
    rows, channels = states.shape[1:]
    halves, block_len, wide = kv_blocks.shape[1:]

    def state_at(m):
        return pl.BlockSpec((1, rows, channels), lambda i, h, s, b: (jnp.maximum(s[h[0] * 6 + m * 3], 0), 0, 0))

    def block_at(m, j):
        return pl.BlockSpec(
            (1, halves, block_len, wide),
            lambda i, h, s, b: (jnp.maximum(b[h[0] * 8 + m * 4 + j], 0), 0, 0, 0),
        )

    packed = (rows, channels + 2 * halves * wide)
    return pl.pallas_call(
        leave_kernel,
        out_shape=[jax.ShapeDtypeStruct(packed, states.dtype)] * 2,
        grid_spec=pltpu.PrefetchScalarGridSpec(
            num_scalar_prefetch=3,
            grid=(1,),
            in_specs=[state_at(0), state_at(1), block_at(0, 0), block_at(0, 1), block_at(1, 0), block_at(1, 1)],
            out_specs=[pl.BlockSpec(packed, lambda i, h, s, b: (0, 0))] * 2,
        ),
        compiler_params=pltpu.CompilerParams(vmem_limit_bytes=12 << 20),
        name="leave",
    )(here, slots, blocks, states, states, kv_blocks, kv_blocks, kv_blocks, kv_blocks)


def clear_kernel(here, slots, blocks, states, cache, new_states, new_cache):
    me = here[0]
    new_states[...] = states[...]
    new_cache[...] = cache[...]
    for m in range(2):
        slot = slots[me * 6 + m * 3]

        @pl.when(slot >= 0)
        def _(slot=slot):
            new_states[slot] = jnp.zeros(states.shape[1:], states.dtype)

        for j in range(2):
            block = blocks[me * 8 + m * 4 + j]

            @pl.when(block >= 0)
            def _(block=block):
                new_cache[block] = jnp.zeros(cache.shape[1:], cache.dtype)


def cleared(here, slots, blocks, states, kv_blocks):
    def all_of(item):
        return pl.BlockSpec(item.shape, lambda i, *_: (0,) * item.ndim)

    return pl.pallas_call(
        clear_kernel,
        out_shape=[jax.ShapeDtypeStruct(v.shape, v.dtype) for v in (states, kv_blocks)],
        grid_spec=pltpu.PrefetchScalarGridSpec(
            num_scalar_prefetch=3,
            grid=(1,),
            in_specs=[all_of(states), all_of(kv_blocks)],
            out_specs=[all_of(states), all_of(kv_blocks)],
        ),
        compiler_params=pltpu.CompilerParams(vmem_limit_bytes=16 << 20),
        name="clear",
    )(here, slots, blocks, states, kv_blocks)


def plan_of(plan_slots, plan_len, plan_blocks):
    ranks = plan_slots.shape[0]
    here = lax.axis_index(RANK).astype(jnp.int32)
    rank_line = jnp.arange(ranks, dtype=jnp.int32)
    live = plan_slots[:, :, 0] >= 0
    span = jnp.where(live, (plan_slots[:, :, 1] - rank_line[:, None]) % ranks, 0)
    far = jnp.max(span, axis=0)
    return here.reshape(1), far, plan_slots.reshape(-1), plan_blocks.reshape(-1), plan_len.reshape(-1)


def patch_kernel(ranks, here, far, slots, blocks, lens, pay0, pay1, _, __, new_states, new_cache, kept, sems):
    channels = new_states.shape[2]
    halves, block_len, wide = new_cache.shape[1:]
    row = lax.broadcasted_iota(jnp.int32, (block_len, wide), 0)
    moves = []
    for m, pay in enumerate((pay0, pay1)):
        sender = lax.rem(here[0] - far[m] + ranks, ranks)
        live = slots[sender * 6 + m * 3] >= 0
        place = jnp.where(live, slots[sender * 6 + m * 3 + 2], 0)
        length = lens[sender * 2 + m]
        copy = pltpu.make_async_copy(pay.at[:, pl.ds(0, channels)], new_states.at[place], sems.at[m * 3])
        moves.append((live, copy))
        pl.when(live)(copy.start)
        for j in range(2):
            spot = blocks[sender * 8 + m * 4 + 2 + j]
            held = live & (spot >= 0)
            for k in range(halves):
                at = channels + (j * halves + k) * wide
                block = pay[:, at : at + wide]
                kept[m * 2 + j, k] = jnp.where(row + j * block_len < length, block, jnp.zeros_like(block))
            copy = pltpu.make_async_copy(
                kept.at[m * 2 + j], new_cache.at[jnp.where(held, spot, 0)], sems.at[m * 3 + 1 + j]
            )
            moves.append((held, copy))
            pl.when(held)(copy.start)
    for held, copy in moves:
        pl.when(held)(copy.wait)


def patched(here, far, slots, blocks, lens, pay0, pay1, new_states, new_cache, ranks):
    anywhere = pl.BlockSpec(memory_space=pltpu.HBM)
    return pl.pallas_call(
        functools.partial(patch_kernel, ranks),
        out_shape=[jax.ShapeDtypeStruct(v.shape, v.dtype) for v in (new_states, new_cache)],
        grid_spec=pltpu.PrefetchScalarGridSpec(
            num_scalar_prefetch=5,
            grid=(1,),
            in_specs=[pl.BlockSpec(pay0.shape, lambda i, *_: (0, 0))] * 2 + [anywhere] * 2,
            out_specs=[anywhere, anywhere],
            scratch_shapes=[pltpu.VMEM((4,) + new_cache.shape[1:], new_cache.dtype), pltpu.SemaphoreType.DMA((6,))],
        ),
        input_output_aliases={7: 0, 8: 1},
        compiler_params=pltpu.CompilerParams(vmem_limit_bytes=12 << 20),
        name="patch",
    )(here, far, slots, blocks, lens, pay0, pay1, new_states, new_cache)


def rows_kernel(blocks, rows):
    for i in range(blocks.shape[0]):
        rows[CAP * i : CAP * (i + 1)] = blocks[i]


def rows_from(blocks):
    count, cap, width = blocks.shape
    return pl.pallas_call(
        rows_kernel,
        out_shape=jax.ShapeDtypeStruct((count * cap, width), blocks.dtype),
        in_specs=[pl.BlockSpec(memory_space=pltpu.VMEM)],
        out_specs=pl.BlockSpec(memory_space=pltpu.VMEM),
        compiler_params=pltpu.CompilerParams(vmem_limit_bytes=12 << 20),
        name="rows",
    )(blocks)


def sum_kernel(count, kept, back, *refs):
    total = kept[...] + back[...].astype(jnp.float32)
    for i in range(count):
        total = total + refs[i][...].astype(jnp.float32)
    total = total.astype(jnp.bfloat16)
    out = refs[count]
    if len(out.shape) == 2:
        out[...] = total
    else:
        for i in range(out.shape[0]):
            out[i] = total[CAP * i : CAP * (i + 1)]


def summed(kept, back, at, rows, *arrived, blocks=False):
    width = kept.shape[1]
    piece = pl.BlockSpec((rows, width), lambda i: (at, 0))
    whole = pl.BlockSpec((rows, width), lambda i: (0, 0))
    shape = (rows // CAP, CAP, width) if blocks else (rows, width)
    return pl.pallas_call(
        functools.partial(sum_kernel, len(arrived)),
        out_shape=jax.ShapeDtypeStruct(shape, jnp.bfloat16),
        grid=(1,),
        in_specs=[piece, piece] + [whole] * len(arrived),
        out_specs=pl.BlockSpec(shape, lambda i: (0,) * len(shape)),
        compiler_params=pltpu.CompilerParams(vmem_limit_bytes=12 << 20),
        name="sums",
    )(kept, back, *arrived)


def mix_kernel(rows, weights, returned, out):
    mixed = []
    for t in range(out.shape[0]):
        total = 0
        for k in range(2):
            row = rows[2 * t + k]
            e, slot = row // CAP, row % CAP
            both = returned[XH * e].astype(jnp.float32)
            for x in range(1, XH):
                both = both + returned[XH * e + x].astype(jnp.float32)
            picked = jnp.where(slot == 0, both[0:1], both[1:2])
            total = total + weights[2 * t + k] * picked
        mixed.append(total)
    out[...] = jnp.concatenate(mixed, axis=0).astype(out.dtype)


def mixed_of(rows, weights, returned, count):
    width = returned.shape[2]
    return pl.pallas_call(
        mix_kernel,
        out_shape=jax.ShapeDtypeStruct((count, width), returned.dtype),
        in_specs=[pl.BlockSpec(memory_space=pltpu.SMEM)] * 2 + [pl.BlockSpec(memory_space=pltpu.VMEM)],
        out_specs=pl.BlockSpec(memory_space=pltpu.VMEM),
        compiler_params=pltpu.CompilerParams(vmem_limit_bytes=12 << 20),
        name="mix",
    )(rows, weights, returned)


def expert_kernel(count, *refs):
    chunks, (gate_w, up_w, down_w, own, other) = refs[:count], refs[count:]
    rows = jnp.concatenate([chunk[...] for chunk in chunks], axis=0)
    gate = jnp.dot(rows, gate_w[0], preferred_element_type=jnp.float32)
    up = jnp.dot(rows, up_w[0], preferred_element_type=jnp.float32)
    hidden = (gate / (1 + jnp.exp(-gate)) * up).astype(jnp.bfloat16)
    half = own.shape[0]
    tile = 512
    for at in range(0, own.shape[1], tile):
        out = jnp.dot(hidden, down_w[0, :, at : at + tile], preferred_element_type=jnp.float32)
        own[:, at : at + tile] = out[:half]
        other[:, at : at + tile] = out[half:].astype(jnp.bfloat16)


def experts_of(mine, theirs, w_gate, w_up, w_down):
    chunks = list(mine) + list(theirs)
    part, width = chunks[0].shape
    units = w_gate.shape[2]
    half = part * len(mine)
    return pl.pallas_call(
        functools.partial(expert_kernel, len(chunks)),
        out_shape=[
            jax.ShapeDtypeStruct((half, width), jnp.float32),
            jax.ShapeDtypeStruct((half, width), jnp.bfloat16),
        ],
        grid=(1,),
        in_specs=[pl.BlockSpec(memory_space=pltpu.VMEM)] * (len(chunks) + 3),
        out_specs=[pl.BlockSpec((half, width), lambda i: (0, 0))] * 2,
        compiler_params=pltpu.CompilerParams(vmem_limit_bytes=12 << 20),
        cost_estimate=pl.CostEstimate(
            flops=12 * half * width * units,
            transcendentals=2 * half * units,
            bytes_accessed=10 * half * width,
        ),
        name="experts",
    )(*chunks, w_gate, w_up, w_down)


def fetch_kernel(*refs):
    count = len(refs) // 2
    sems = refs[-1]
    copies = [pltpu.make_async_copy(refs[i], refs[count + i], sems.at[i]) for i in range(count)]
    for copy in copies:
        copy.start()
    for copy in copies:
        copy.wait()


def fetched(*weights):
    return pl.pallas_call(
        fetch_kernel,
        out_shape=[pltpu.VMEM(w.shape, w.dtype) for w in weights],
        in_specs=[pl.BlockSpec(memory_space=pltpu.HBM)] * len(weights),
        out_specs=[pl.BlockSpec(memory_space=pltpu.VMEM)] * len(weights),
        scratch_shapes=[pltpu.SemaphoreType.DMA((len(weights),))],
        compiler_params=pltpu.CompilerParams(vmem_limit_bytes=44 << 20),
        name="fetch",
    )(*weights)


def local(
    tokens, router, expert_ids, w_gate, w_up, w_down, states, kv_blocks, plan_slots, plan_len, plan_blocks
):
    experts = router.shape[1]
    tok_count, width = tokens.shape
    f32, bf16 = jnp.float32, jnp.bfloat16
    here, far, slots, blocks, lens = plan_of(plan_slots, plan_len, plan_blocks)
    ranks = plan_slots.shape[0]
    flat_ids = expert_ids.reshape(-1)
    onehot = (flat_ids[:, None] == jnp.arange(experts)[None, :]).astype(jnp.int32)
    earlier = jnp.cumsum(onehot, axis=0) - onehot
    slot_of = jnp.sum(earlier * onehot, axis=1)
    target_row = flat_ids * CAP + slot_of
    placer = (jnp.arange(experts * CAP)[:, None] == target_row[None, :]).astype(bf16)
    doubled = jnp.repeat(tokens, 2, axis=0)
    packed = jnp.dot(placer, doubled, preferred_element_type=f32).astype(bf16)
    outgoing = jnp.repeat(packed.reshape(experts, CAP, width), XH, axis=0)
    own = lax.all_to_all(outgoing, COLUMN, split_axis=0, concat_axis=0, tiled=True)
    pay0, pay1 = leaving(here, slots, blocks, states, kv_blocks)
    far, pay0, pay1, lens = lax.optimization_barrier((far, pay0, pay1, lens))
    pay0 = sent_by(pay0, far[0] % Z, ranks)
    own, pay0, pay1, far, lens = lax.optimization_barrier((own, pay0, pay1, far, lens))
    own = rows_from(own)
    part = own.shape[0]
    own, w_gate, w_up, w_down = lax.optimization_barrier((own, w_gate, w_up, w_down))
    kept = {}

    def run_experts(names, mine):
        theirs = [passed(chunk, "c", 1) for chunk in mine]
        ours, sent = experts_of(mine, theirs, w_gate, w_up, w_down)
        sent = passed(sent, "c", 1)
        ours, sent = (pltpu.with_memory_space_constraint(v, pltpu.HBM) for v in (ours, sent))
        for i, name in enumerate(names):
            kept[name] = (ours, sent, i, part)
        return ours

    down, up = passed(own, "z", 1), passed(own, "z", -1)
    w_gate, w_up, w_down = fetched(w_gate, w_up, w_down)
    done = run_experts([0], [own])
    waiting = []
    for step in range(1, Z // 2 + 1):
        down, done = lax.optimization_barrier((down, done))
        names, chunks = [-step] + [name for name, _ in waiting], [down] + [chunk for _, chunk in waiting]
        if step < Z // 2:
            down = passed(down, "z", 1)
        done = run_experts(names, chunks)
        if step < Z // 2:
            up, done = lax.optimization_barrier((up, done))
            waiting = [(step, up)]
            if step < Z // 2 - 1:
                up = passed(up, "z", -1)

    left, right = summed(*kept[-Z // 2]), summed(*kept[Z // 2 - 1])
    left, states, kv_blocks, pay0, pay1 = lax.optimization_barrier((left, states, kv_blocks, pay0, pay1))
    moving = jnp.stack([pay0, pay1])
    new_states, new_cache = cleared(here, slots, blocks, states, kv_blocks)
    for d in range(Z // 2 - 1, -1, -1):
        if d:
            left, moving = lax.optimization_barrier((left, moving))
        left = passed(left, "z", -1)
        if d:
            unit = Z << (Z // 2 - 1 - d)
            moved = passed(moving, RANK, unit)
            left, moved = lax.optimization_barrier((left, moved))
            moving = turned_by(far, moved, moving, unit, d == 1)
            left = summed(*kept[-d], left)
            if d == 1:
                left, tokens, router, expert_ids = lax.optimization_barrier((left, tokens, router, expert_ids))
            right = passed(right, "z", 1)
            if d > 1:
                right = summed(*kept[d - 1], right)
    logits = jnp.dot(tokens.astype(f32), router, precision=lax.Precision.HIGHEST)
    scores = jax.nn.sigmoid(jnp.take_along_axis(logits, expert_ids, axis=1))
    weights = (scores / jnp.sum(scores, axis=1, keepdims=True)).reshape(-1)
    total = summed(*kept[0], left, right, blocks=True)
    total, pay0, pay1, weights, new_states, new_cache = lax.optimization_barrier((total, *moving, weights, new_states, new_cache))
    returned = lax.all_to_all(
        total, COLUMN, split_axis=0, concat_axis=0, tiled=True
    )
    pay1 = sent_by(pay1, far[1] % Z, ranks)
    new_states, new_cache = patched(here, far, slots, blocks, lens, pay0, pay1, new_states, new_cache, ranks)
    returned, new_states, new_cache = lax.optimization_barrier((returned, new_states, new_cache))
    mixed = mixed_of(target_row, weights, returned, tok_count)
    return mixed, new_states, new_cache


def solution(mesh):
    fine = Mesh(mesh.devices.reshape(XL, Y, Z, XH, C), ("xl", "y", "z", "xh", "c"))
    inner = ("xh", "c")
    everyone = RANK + inner
    placed = (
        P(everyone, None),
        P(),
        P(everyone, None),
        P(RANK, None, inner),
        P(RANK, None, inner),
        P(RANK, inner, None),
        P(RANK, None, inner),
        P(RANK, None, None, inner),
        P(),
        P(),
        P(),
    )
    return jax.shard_map(
        local,
        mesh=fine,
        in_specs=placed,
        out_specs=(P(everyone, None), P(RANK, None, inner), P(RANK, None, None, inner)),
        check_vma=False,
    )
```

```python
import functools
import math

import jax
import jax.numpy as jnp
from jax import lax
from jax.experimental import pallas as pl
from jax.experimental.pallas import tpu as pltpu
from jax.sharding import Mesh, PartitionSpec as P

CAP = 2
XL, Y, Z, XH, C = 2, 4, 8, 2, 2
RANK = ("xl", "y", "z")
COLUMN = ("xl", "y", "xh")


def passed(value, axis, steps):
    count = math.prod(lax.axis_size(name) for name in axis) if isinstance(axis, tuple) else lax.axis_size(axis)
    pairs = [(source, (source + steps) % count) for source in range(count)]
    return lax.ppermute(value, axis, pairs)


def sent_by(value, digit, ranks):
    def branch(steps):
        pairs = [(source, (source + steps) % ranks) for source in range(ranks)]
        return lambda item: lax.ppermute(item, RANK, pairs)

    return lax.switch(digit, [lambda item: item] + [branch(steps) for steps in range(1, Z)], value)


def leave_kernel(here, slots, blocks, s0, s1, k00, k01, k10, k11, out0, out1):
    channels = s0.shape[2]
    for state, cache, out in ((s0, (k00, k01), out0), (s1, (k10, k11), out1)):
        out[:, :channels] = state[0]
        at = channels
        for block in cache:
            for k in range(block.shape[1]):
                wide = block.shape[3]
                out[:, at : at + wide] = block[0, k]
                at += wide


def turn_kernel(bit, far, moved, moving, *outs):
    for m in range(2):
        taken = lax.rem(lax.div(far[m], bit), 2) == 1
        value = jnp.where(taken, moved[m], moving[m])
        if len(outs) == 2:
            outs[m][...] = value
        else:
            outs[0][m] = value


def turned_by(far, moved, moving, bit, apart):
    whole = jax.ShapeDtypeStruct(moving.shape, moving.dtype)
    single = jax.ShapeDtypeStruct(moving.shape[1:], moving.dtype)
    vmem = pl.BlockSpec(memory_space=pltpu.VMEM)
    return pl.pallas_call(
        functools.partial(turn_kernel, bit),
        out_shape=[single] * 2 if apart else whole,
        in_specs=[pl.BlockSpec(memory_space=pltpu.SMEM), vmem, vmem],
        out_specs=[vmem] * 2 if apart else vmem,
        compiler_params=pltpu.CompilerParams(vmem_limit_bytes=12 << 20),
        name="turn",
    )(far, moved, moving)


def leaving(here, slots, blocks, states, kv_blocks):
    rows, channels = states.shape[1:]
    halves, block_len, wide = kv_blocks.shape[1:]

    def state_at(m):
        return pl.BlockSpec((1, rows, channels), lambda i, h, s, b: (jnp.maximum(s[h[0] * 6 + m * 3], 0), 0, 0))

    def block_at(m, j):
        return pl.BlockSpec(
            (1, halves, block_len, wide),
            lambda i, h, s, b: (jnp.maximum(b[h[0] * 8 + m * 4 + j], 0), 0, 0, 0),
        )

    packed = (rows, channels + 2 * halves * wide)
    return pl.pallas_call(
        leave_kernel,
        out_shape=[jax.ShapeDtypeStruct(packed, states.dtype)] * 2,
        grid_spec=pltpu.PrefetchScalarGridSpec(
            num_scalar_prefetch=3,
            grid=(1,),
            in_specs=[state_at(0), state_at(1), block_at(0, 0), block_at(0, 1), block_at(1, 0), block_at(1, 1)],
            out_specs=[pl.BlockSpec(packed, lambda i, h, s, b: (0, 0))] * 2,
        ),
        compiler_params=pltpu.CompilerParams(vmem_limit_bytes=12 << 20),
        name="leave",
    )(here, slots, blocks, states, states, kv_blocks, kv_blocks, kv_blocks, kv_blocks)


def clear_kernel(here, slots, blocks, states, cache, new_states, new_cache):
    me = here[0]

    @pl.loop(0, states.shape[0])
    def _(i):
        new_states[i] = states[i]

    @pl.loop(0, cache.shape[0])
    def _(i):
        new_cache[i] = cache[i]

    for m in range(2):
        slot = slots[me * 6 + m * 3]

        @pl.when(slot >= 0)
        def _(slot=slot):
            new_states[slot] = jnp.zeros(states.shape[1:], states.dtype)

        for j in range(2):
            block = blocks[me * 8 + m * 4 + j]

            @pl.when(block >= 0)
            def _(block=block):
                new_cache[block] = jnp.zeros(cache.shape[1:], cache.dtype)


def cleared(here, slots, blocks, states, kv_blocks):
    def all_of(item):
        return pl.BlockSpec(item.shape, lambda i, *_: (0,) * item.ndim)

    return pl.pallas_call(
        clear_kernel,
        out_shape=[jax.ShapeDtypeStruct(v.shape, v.dtype) for v in (states, kv_blocks)],
        grid_spec=pltpu.PrefetchScalarGridSpec(
            num_scalar_prefetch=3,
            grid=(1,),
            in_specs=[all_of(states), all_of(kv_blocks)],
            out_specs=[all_of(states), all_of(kv_blocks)],
        ),
        compiler_params=pltpu.CompilerParams(vmem_limit_bytes=16 << 20),
        name="clear",
    )(here, slots, blocks, states, kv_blocks)


def plan_of(plan_slots, plan_len, plan_blocks):
    ranks = plan_slots.shape[0]
    here = lax.axis_index(RANK).astype(jnp.int32)
    rank_line = jnp.arange(ranks, dtype=jnp.int32)
    live = plan_slots[:, :, 0] >= 0
    span = jnp.where(live, (plan_slots[:, :, 1] - rank_line[:, None]) % ranks, 0)
    far = jnp.max(span, axis=0)
    return here.reshape(1), far, plan_slots.reshape(-1), plan_blocks.reshape(-1), plan_len.reshape(-1)


def patch_kernel(ranks, here, far, slots, blocks, lens, pay0, pay1, _, __, new_states, new_cache, kept, sems):
    channels = new_states.shape[2]
    halves, block_len, wide = new_cache.shape[1:]
    row = lax.broadcasted_iota(jnp.int32, (block_len, wide), 0)
    moves = []
    for m, pay in enumerate((pay0, pay1)):
        sender = lax.rem(here[0] - far[m] + ranks, ranks)
        live = slots[sender * 6 + m * 3] >= 0
        place = jnp.where(live, slots[sender * 6 + m * 3 + 2], 0)
        length = lens[sender * 2 + m]
        copy = pltpu.make_async_copy(pay.at[:, pl.ds(0, channels)], new_states.at[place], sems.at[m * 3])
        moves.append((live, copy))
        pl.when(live)(copy.start)
        for j in range(2):
            spot = blocks[sender * 8 + m * 4 + 2 + j]
            held = live & (spot >= 0)
            for k in range(halves):
                at = channels + (j * halves + k) * wide
                block = pay[:, at : at + wide]
                kept[m * 2 + j, k] = jnp.where(row + j * block_len < length, block, jnp.zeros_like(block))
            copy = pltpu.make_async_copy(
                kept.at[m * 2 + j], new_cache.at[jnp.where(held, spot, 0)], sems.at[m * 3 + 1 + j]
            )
            moves.append((held, copy))
            pl.when(held)(copy.start)
    for held, copy in moves:
        pl.when(held)(copy.wait)


def patched(here, far, slots, blocks, lens, pay0, pay1, new_states, new_cache, ranks):
    anywhere = pl.BlockSpec(memory_space=pltpu.HBM)
    return pl.pallas_call(
        functools.partial(patch_kernel, ranks),
        out_shape=[jax.ShapeDtypeStruct(v.shape, v.dtype) for v in (new_states, new_cache)],
        grid_spec=pltpu.PrefetchScalarGridSpec(
            num_scalar_prefetch=5,
            grid=(1,),
            in_specs=[pl.BlockSpec(pay0.shape, lambda i, *_: (0, 0))] * 2 + [anywhere] * 2,
            out_specs=[anywhere, anywhere],
            scratch_shapes=[pltpu.VMEM((4,) + new_cache.shape[1:], new_cache.dtype), pltpu.SemaphoreType.DMA((6,))],
        ),
        input_output_aliases={7: 0, 8: 1},
        compiler_params=pltpu.CompilerParams(vmem_limit_bytes=12 << 20),
        name="patch",
    )(here, far, slots, blocks, lens, pay0, pay1, new_states, new_cache)


def rows_kernel(blocks, rows):
    for i in range(blocks.shape[0]):
        rows[CAP * i : CAP * (i + 1)] = blocks[i]


def rows_from(blocks):
    count, cap, width = blocks.shape
    return pl.pallas_call(
        rows_kernel,
        out_shape=jax.ShapeDtypeStruct((count * cap, width), blocks.dtype),
        in_specs=[pl.BlockSpec(memory_space=pltpu.VMEM)],
        out_specs=pl.BlockSpec(memory_space=pltpu.VMEM),
        compiler_params=pltpu.CompilerParams(vmem_limit_bytes=12 << 20),
        name="rows",
    )(blocks)


def sum_kernel(count, kept, back, *refs):
    out = refs[count]
    tile = 512

    @pl.loop(0, kept.shape[1] // tile)
    def _(n):
        part = pl.ds(pl.multiple_of(n * tile, tile), tile)
        total = kept[:, part] + back[:, part].astype(jnp.float32)
        for i in range(count):
            total = total + refs[i][:, part].astype(jnp.float32)
        total = total.astype(jnp.bfloat16)
        if len(out.shape) == 2:
            out[:, part] = total
        else:
            for i in range(out.shape[0]):
                out[i, :, part] = total[CAP * i : CAP * (i + 1)]


def summed(kept, back, at, rows, *arrived, blocks=False):
    width = kept.shape[1]
    piece = pl.BlockSpec((rows, width), lambda i: (at, 0))
    whole = pl.BlockSpec((rows, width), lambda i: (0, 0))
    shape = (rows // CAP, CAP, width) if blocks else (rows, width)
    return pl.pallas_call(
        functools.partial(sum_kernel, len(arrived)),
        out_shape=jax.ShapeDtypeStruct(shape, jnp.bfloat16),
        grid=(1,),
        in_specs=[piece, piece] + [whole] * len(arrived),
        out_specs=pl.BlockSpec(shape, lambda i: (0,) * len(shape)),
        compiler_params=pltpu.CompilerParams(vmem_limit_bytes=12 << 20),
        name="sums",
    )(kept, back, *arrived)


def mix_kernel(rows, weights, returned, out):
    mixed = []
    for t in range(out.shape[0]):
        total = 0
        for k in range(2):
            row = rows[2 * t + k]
            e, slot = row // CAP, row % CAP
            both = returned[XH * e].astype(jnp.float32)
            for x in range(1, XH):
                both = both + returned[XH * e + x].astype(jnp.float32)
            picked = jnp.where(slot == 0, both[0:1], both[1:2])
            total = total + weights[2 * t + k] * picked
        mixed.append(total)
    out[...] = jnp.concatenate(mixed, axis=0).astype(out.dtype)


def mixed_of(rows, weights, returned, count):
    width = returned.shape[2]
    return pl.pallas_call(
        mix_kernel,
        out_shape=jax.ShapeDtypeStruct((count, width), returned.dtype),
        in_specs=[pl.BlockSpec(memory_space=pltpu.SMEM)] * 2 + [pl.BlockSpec(memory_space=pltpu.VMEM)],
        out_specs=pl.BlockSpec(memory_space=pltpu.VMEM),
        compiler_params=pltpu.CompilerParams(vmem_limit_bytes=12 << 20),
        name="mix",
    )(rows, weights, returned)


def expert_kernel(count, *refs):
    chunks, (gate_w, up_w, down_w, own, other, gate, up, hidden) = refs[:count], refs[count:]
    half, width = own.shape
    tile = 512
    gate[...] = jnp.zeros_like(gate)
    up[...] = jnp.zeros_like(up)

    @pl.loop(0, width // tile)
    def _(k):
        part = pl.ds(pl.multiple_of(k * tile, tile), tile)
        rows = jnp.concatenate([chunk[:, part] for chunk in chunks], axis=0)
        gate[...] += jnp.dot(rows, gate_w[0, part], preferred_element_type=jnp.float32)
        up[...] += jnp.dot(rows, up_w[0, part], preferred_element_type=jnp.float32)

    g = gate[...]
    hidden[...] = (g / (1 + jnp.exp(-g)) * up[...]).astype(jnp.bfloat16)

    @pl.loop(0, width // tile)
    def _(n):
        part = pl.ds(pl.multiple_of(n * tile, tile), tile)
        out = jnp.dot(hidden[...], down_w[0, :, part], preferred_element_type=jnp.float32)
        own[:, part] = out[:half]
        other[:, part] = out[half:].astype(jnp.bfloat16)


def experts_of(mine, theirs, w_gate, w_up, w_down):
    chunks = list(mine) + list(theirs)
    part, width = chunks[0].shape
    units = w_gate.shape[2]
    half = part * len(mine)
    return pl.pallas_call(
        functools.partial(expert_kernel, len(chunks)),
        out_shape=[
            jax.ShapeDtypeStruct((half, width), jnp.float32),
            jax.ShapeDtypeStruct((half, width), jnp.bfloat16),
        ],
        grid=(1,),
        in_specs=[pl.BlockSpec(memory_space=pltpu.VMEM)] * (len(chunks) + 3),
        out_specs=[pl.BlockSpec((half, width), lambda i: (0, 0))] * 2,
        scratch_shapes=[
            pltpu.VMEM((2 * half, units), jnp.float32),
            pltpu.VMEM((2 * half, units), jnp.float32),
            pltpu.VMEM((2 * half, units), jnp.bfloat16),
        ],
        compiler_params=pltpu.CompilerParams(vmem_limit_bytes=12 << 20),
        cost_estimate=pl.CostEstimate(
            flops=12 * half * width * units,
            transcendentals=2 * half * units,
            bytes_accessed=10 * half * width,
        ),
        name="experts",
    )(*chunks, w_gate, w_up, w_down)


def fetch_kernel(*refs):
    count = len(refs) // 2
    sems = refs[-1]
    copies = [pltpu.make_async_copy(refs[i], refs[count + i], sems.at[i]) for i in range(count)]
    for copy in copies:
        copy.start()
    for copy in copies:
        copy.wait()


def fetched(*weights):
    return pl.pallas_call(
        fetch_kernel,
        out_shape=[pltpu.VMEM(w.shape, w.dtype) for w in weights],
        in_specs=[pl.BlockSpec(memory_space=pltpu.HBM)] * len(weights),
        out_specs=[pl.BlockSpec(memory_space=pltpu.VMEM)] * len(weights),
        scratch_shapes=[pltpu.SemaphoreType.DMA((len(weights),))],
        compiler_params=pltpu.CompilerParams(vmem_limit_bytes=44 << 20),
        name="fetch",
    )(*weights)


def local(
    tokens, router, expert_ids, w_gate, w_up, w_down, states, kv_blocks, plan_slots, plan_len, plan_blocks
):
    experts = router.shape[1]
    tok_count, width = tokens.shape
    f32, bf16 = jnp.float32, jnp.bfloat16
    here, far, slots, blocks, lens = plan_of(plan_slots, plan_len, plan_blocks)
    ranks = plan_slots.shape[0]
    flat_ids = expert_ids.reshape(-1)
    onehot = (flat_ids[:, None] == jnp.arange(experts)[None, :]).astype(jnp.int32)
    earlier = jnp.cumsum(onehot, axis=0) - onehot
    slot_of = jnp.sum(earlier * onehot, axis=1)
    target_row = flat_ids * CAP + slot_of
    placer = (jnp.arange(experts * CAP)[:, None] == target_row[None, :]).astype(bf16)
    doubled = jnp.repeat(tokens, 2, axis=0)
    packed = jnp.dot(placer, doubled, preferred_element_type=f32).astype(bf16)
    outgoing = jnp.repeat(packed.reshape(experts, CAP, width), XH, axis=0)
    own = lax.all_to_all(outgoing, COLUMN, split_axis=0, concat_axis=0, tiled=True)
    pay0, pay1 = leaving(here, slots, blocks, states, kv_blocks)
    far, pay0, pay1, lens = lax.optimization_barrier((far, pay0, pay1, lens))
    pay0 = sent_by(pay0, far[0] % Z, ranks)
    own, pay0, pay1, far, lens = lax.optimization_barrier((own, pay0, pay1, far, lens))
    own = rows_from(own)
    part = own.shape[0]
    own, w_gate, w_up, w_down = lax.optimization_barrier((own, w_gate, w_up, w_down))
    kept = {}

    def run_experts(names, mine):
        theirs = [passed(chunk, "c", 1) for chunk in mine]
        ours, sent = experts_of(mine, theirs, w_gate, w_up, w_down)
        sent = passed(sent, "c", 1)
        ours, sent = (pltpu.with_memory_space_constraint(v, pltpu.HBM) for v in (ours, sent))
        for i, name in enumerate(names):
            kept[name] = (ours, sent, i, part)
        return ours

    down, up = passed(own, "z", 1), passed(own, "z", -1)
    w_gate, w_up, w_down = fetched(w_gate, w_up, w_down)
    done = run_experts([0], [own])
    waiting = []
    for step in range(1, Z // 2 + 1):
        down, done = lax.optimization_barrier((down, done))
        names, chunks = [-step] + [name for name, _ in waiting], [down] + [chunk for _, chunk in waiting]
        if step < Z // 2:
            down = passed(down, "z", 1)
        done = run_experts(names, chunks)
        if step < Z // 2:
            up, done = lax.optimization_barrier((up, done))
            waiting = [(step, up)]
            if step < Z // 2 - 1:
                up = passed(up, "z", -1)

    left, right = summed(*kept[-Z // 2]), summed(*kept[Z // 2 - 1])
    left, states, kv_blocks, pay0, pay1 = lax.optimization_barrier((left, states, kv_blocks, pay0, pay1))
    moving = jnp.stack([pay0, pay1])
    new_states, new_cache = cleared(here, slots, blocks, states, kv_blocks)
    for d in range(Z // 2 - 1, -1, -1):
        if d:
            left, moving = lax.optimization_barrier((left, moving))
        left = passed(left, "z", -1)
        if d:
            unit = Z << (Z // 2 - 1 - d)
            moved = passed(moving, RANK, unit)
            left, moved = lax.optimization_barrier((left, moved))
            moving = turned_by(far, moved, moving, unit, d == 1)
            left = summed(*kept[-d], left)
            if d == 1:
                left, tokens, router, expert_ids = lax.optimization_barrier((left, tokens, router, expert_ids))
            right = passed(right, "z", 1)
            if d > 1:
                right = summed(*kept[d - 1], right)
    logits = jnp.dot(tokens.astype(f32), router, precision=lax.Precision.HIGHEST)
    scores = jax.nn.sigmoid(jnp.take_along_axis(logits, expert_ids, axis=1))
    weights = (scores / jnp.sum(scores, axis=1, keepdims=True)).reshape(-1)
    total = summed(*kept[0], left, right, blocks=True)
    total, pay0, pay1, weights, new_states, new_cache = lax.optimization_barrier((total, *moving, weights, new_states, new_cache))
    returned = lax.all_to_all(
        total, COLUMN, split_axis=0, concat_axis=0, tiled=True
    )
    pay1 = sent_by(pay1, far[1] % Z, ranks)
    new_states, new_cache = patched(here, far, slots, blocks, lens, pay0, pay1, new_states, new_cache, ranks)
    returned, new_states, new_cache = lax.optimization_barrier((returned, new_states, new_cache))
    mixed = mixed_of(target_row, weights, returned, tok_count)
    return mixed, new_states, new_cache


def solution(mesh):
    fine = Mesh(mesh.devices.reshape(XL, Y, Z, XH, C), ("xl", "y", "z", "xh", "c"))
    inner = ("xh", "c")
    everyone = RANK + inner
    placed = (
        P(everyone, None),
        P(),
        P(everyone, None),
        P(RANK, None, inner),
        P(RANK, None, inner),
        P(RANK, inner, None),
        P(RANK, None, inner),
        P(RANK, None, None, inner),
        P(),
        P(),
        P(),
    )
    return jax.shard_map(
        local,
        mesh=fine,
        in_specs=placed,
        out_specs=(P(everyone, None), P(RANK, None, inner), P(RANK, None, None, inner)),
        check_vma=False,
    )
```
